32 devices in a mesh: grp: 2 (over y), sta: 16 (over z, x, core).
Axes of the slice: x: 2, y: 2, z: 4, core: 2. Of those that a mesh axis runs over, the one named last changes fastest.
Arguments:
- traces: bfloat16 [32, 2048], P(('grp', 'sta')), parts along dimension 0, may hold values from -6 to 6
- templates: bfloat16 [16, 32, 512], P(None, ('grp', 'sta')), parts along dimension 1, may hold values from -6 to 6
- moveouts: int32 [16, 32], P(None, ('grp', 'sta')), parts along dimension 1, may hold values from 0 to 511
- channel_mask: int32 [32], P(('grp', 'sta')), parts along dimension 0, may hold values 0 or 1
- owner_slot: int32 [16], replicated, may hold values from 0 to 15, each once
Outputs:
- updated_templates: bfloat16 [16, 32, 512], P(None, ('grp', 'sta')), parts along dimension 1
- owner_weights: bfloat16 [32, 1024], P(('grp', 'sta')), parts along dimension 0
The draws below stay inside these ranges and needn't reach their ends.
There are 2 independent parts, one for each index of `grp`. The reference program is written for one: setup_inputs(seed, part) draws one part's arguments, and reference() takes and returns one part's arrays. A program takes and returns all parts, laid end to end along the dimension named above; an argument that names none is the same for every part. Nothing has to cross between parts.
Inputs may be any that keep to these rules, and one draw needn't show every extreme that they name: owner_slot names each row of 0 to 15 once.
All inputs are finite; a program needn't handle non-finite values. No bound on the sum of `channel_mask` on one device may be relied on, other than what follows from the above.
Results may differ from the reference program's by a relative error of at most 0.0057.
Values may be sent and summed in bfloat16 or wider, within the bound.
No kernel may reach another device: no remote copies, remote signals or barrier semaphores. Data moves between devices by JAX's collectives and lax.ppermute only.
A program may use at most 64 MiB of HBM per device.

```python
import jax
import jax.numpy as jnp
from jax import lax

LEN = 512
MOVE = 512
NT = 1024
WIN = 2048
STATIONS = 16
TEMPLATES = 16


def plant(drawn, own_key, low, high):
    longest = drawn.shape.index(max(drawn.shape))
    spots = []
    for shift in (0, 1):
        where = [jax.random.randint(jax.random.fold_in(own_key, axis), (), 0, length) for axis, length in enumerate(drawn.shape)]
        where[longest] = (where[longest] + shift) % drawn.shape[longest]
        spots.append(tuple(where))
    return drawn.at[spots[0]].set(low).at[spots[1]].set(high)


def block_levels(rng, dims, pieces, least, high):
    factor_of = 1.0
    for position, parts in pieces:
        heights = jax.random.uniform(jax.random.fold_in(jax.random.fold_in(rng, 6), position), (parts,), jnp.float32, least / len(pieces), high / len(pieces))
        factor_of = factor_of * jnp.repeat(jnp.exp(heights), dims[position] // parts).reshape((-1,) + (1,) * (len(dims) - 1 - position))
    return factor_of


def centred(own_key, shape, deviation, bound, shards=(), kind=jnp.bfloat16):
    level = block_levels(own_key, shape, shards, -0.22, 0.18) if shards else 1.0
    drawn = jax.random.normal(own_key, shape, jnp.float32) * deviation * level
    return jnp.minimum(jnp.maximum(drawn, -bound), bound).astype(kind)


def setup_inputs(seed: int = 0, part: int = 0) -> dict:
    keys = jax.random.split(jax.random.key(seed), 6)
    part_splits = jax.random.split(jax.random.fold_in(keys[5], part), 6)
    traces = centred(part_splits[0], (STATIONS, WIN), 1.0, 6.0, ((0, 16),))
    templates = centred(part_splits[1], (TEMPLATES, STATIONS, LEN), 1.0, 6.0, ((1, 16),))
    moveouts = plant(jax.random.randint(part_splits[2], (TEMPLATES, STATIONS), 0, MOVE), jax.random.fold_in(part_splits[2], 1), 0, MOVE - 1).astype(jnp.int32)
    channel_mask = plant((jax.random.randint(part_splits[3], (STATIONS,), 0, 4) < 3).astype(jnp.int32), jax.random.fold_in(part_splits[3], 1), 0, 1)
    owner_slot = jax.random.permutation(keys[4], TEMPLATES).astype(jnp.int32)
    return dict(traces=traces, templates=templates, moveouts=moveouts, channel_mask=channel_mask, owner_slot=owner_slot)


def correlate(record, kernels):
    output = lax.conv_general_dilated(record[None, None, :], kernels[:, None, :], (1,), 'VALID', dimension_numbers=('NCH', 'OIH', 'NCH'), precision=lax.Precision.HIGHEST, preferred_element_type=jnp.float32)
    return output[0]

def aligned_rows(correlogram, moveout):
    return jax.vmap(lambda values, offset: lax.dynamic_slice_in_dim(values, offset, NT))(correlogram, moveout)

def shifted_rows(weights, moveout):
    padded = jnp.pad(weights, ((0, 0), (MOVE, MOVE)))
    return jax.vmap(lambda values, offset: lax.dynamic_slice_in_dim(values, MOVE - offset, NT + MOVE))(padded, moveout)

def reference(traces, templates, moveouts, channel_mask, owner_slot):
    widened = templates.astype(jnp.float32)
    normed = (widened * lax.rsqrt(lax.optimization_barrier(jnp.sum(widened * widened, axis=2, keepdims=True)) + 1e-06)).astype(jnp.bfloat16)
    records = traces.astype(jnp.float32)
    kernels_all = jnp.transpose(normed, (1, 0, 2)).astype(jnp.float32)
    station_moves = jnp.transpose(moveouts)
    usable = channel_mask.astype(jnp.float32)

    def forward(running, station):
        record, kernels, moveout, weight = station
        return (running + aligned_rows(correlate(record, kernels), moveout) * weight, None)
    partial_value, ignored = lax.scan(forward, jnp.zeros((TEMPLATES, NT), jnp.float32), (records, kernels_all, station_moves, usable))
    count = jnp.sum(usable)
    stack = partial_value * lax.rsqrt(jnp.maximum(count, 1.0))
    weights = (stack * stack * stack).astype(jnp.bfloat16)
    owner_weights = jnp.zeros_like(weights).at[owner_slot].set(weights)
    widened_weights = weights.astype(jnp.float32)

    def adjoint(station):
        record, moveout, usable_flag, initial = station
        update = correlate(record, shifted_rows(widened_weights, moveout))[:, :LEN]
        normal_update = update * lax.rsqrt(lax.optimization_barrier(jnp.mean(update * update, axis=1, keepdims=True)) + 1e-06)
        return jnp.where(usable_flag == 1, normal_update, initial.astype(jnp.float32)).astype(jnp.bfloat16)
    updated = lax.map(adjoint, (records, station_moves, channel_mask, jnp.transpose(templates, (1, 0, 2))))
    return (jnp.transpose(updated, (1, 0, 2)), owner_weights)
```

```python
import functools

import jax
import jax.numpy as jnp
from jax import lax
from jax.experimental import pallas as pl
from jax.experimental.pallas import tpu as pltpu
from jax.sharding import PartitionSpec as P

MOVE = 512
LANES = 128


def column(row):
    n = row.shape[1]
    wide = jnp.broadcast_to(row.astype(jnp.float32), (n, n))
    here = lax.broadcasted_iota(jnp.int32, (n, n), 0) == lax.broadcasted_iota(jnp.int32, (n, n), 1)
    return jnp.sum(jnp.where(here, wide, 0.0), axis=1, keepdims=True).astype(jnp.int32)


def blocks_of(value):
    return [value[:, i : i + LANES] for i in range(0, value.shape[1], LANES)]


def hankel(trace):
    win = trace.shape[1]
    base = jnp.broadcast_to(trace.astype(jnp.float32), (8, win))
    row = lax.broadcasted_iota(jnp.int32, (8, win), 0)
    for step in (1, 2, 4):
        base = jnp.where((row & step) != 0, pltpu.roll(base, win - step, 1), base)
    rows = [base] + [pltpu.roll(base, win - step, 1) for step in range(8, LANES, 8)]
    return jnp.concatenate(rows, axis=0).astype(jnp.bfloat16)


def forward_kernel(span, mask_ref, trace_ref, templates_ref, moves_ref, partial_ref, hankel_ref):
    count, length = templates_ref.shape
    hankel_ref[...] = hankel(trace_ref[...])
    widened = templates_ref[...].astype(jnp.float32)
    normed = widened * lax.rsqrt(jnp.sum(widened * widened, axis=1, keepdims=True) + 1e-06)
    pieces = blocks_of(normed.astype(jnp.bfloat16))
    lags = span + MOVE
    wide = lags + length - LANES
    products = jnp.dot(
        jnp.concatenate(pieces, axis=0),
        hankel_ref[:, :wide],
        preferred_element_type=jnp.float32,
    )
    found = []
    for lag in range(0, lags, LANES):
        terms = [
            products[i * count : (i + 1) * count, lag + i * LANES : lag + (i + 1) * LANES]
            for i in range(len(pieces))
        ]
        found.append(functools.reduce(jnp.add, terms))
    moves = jnp.broadcast_to(column(moves_ref[...]), (count, LANES))
    whole, rest = moves // LANES, moves % LANES
    lane = lax.broadcasted_iota(jnp.int32, (count, LANES), 1)
    source = (lane + rest) % LANES
    inside = lane + rest < LANES
    turned = []
    for j in range(span // LANES + 1):
        near = found[j]
        for h in range(1, MOVE // LANES):
            if j + h < len(found):
                near = jnp.where(whole == h, found[j + h], near)
        turned.append(jnp.take_along_axis(near, source, axis=1))
    weight = mask_ref[0].astype(jnp.float32)
    for j in range(span // LANES):
        partial_ref[:, j * LANES : (j + 1) * LANES] = (
            jnp.where(inside, turned[j], turned[j + 1]) * weight
        )
    partial_ref[:, span:] = jnp.full((count, LANES), weight, jnp.float32)


def adjoint_kernel(
    span, owned, mask_ref, total_ref, hankel_ref, templates_ref, moves_ref, slots_ref,
    updated_ref, own_ref, spread,
):
    count, length = templates_ref.shape
    usable = jnp.max(total_ref[:, span:], axis=1, keepdims=True)
    stack = total_ref[:, :span] * lax.rsqrt(jnp.maximum(usable, 1.0))
    weights = (stack * stack * stack).astype(jnp.bfloat16)
    wide = weights.astype(jnp.float32)
    slots = jnp.broadcast_to(column(slots_ref[...]), (count, span))
    first = lax.axis_index("sta") * owned
    for j in range(owned):
        mine = jnp.sum(jnp.where(slots == first + j, wide, 0.0), axis=0, keepdims=True)
        own_ref[j : j + 1, :] = mine.astype(jnp.bfloat16)
    moves = jnp.broadcast_to(column(moves_ref[...]), (count, LANES))
    whole, rest = moves // LANES, moves % LANES
    lane = lax.broadcasted_iota(jnp.int32, (count, LANES), 1)
    source = (lane + LANES - rest) % LANES
    inside = lane >= rest
    zero = jnp.zeros((count, LANES), jnp.float32)
    turned = [zero] + [jnp.take_along_axis(b, source, axis=1) for b in blocks_of(wide)] + [zero]
    shifted = [jnp.where(inside, turned[j + 1], turned[j]) for j in range(len(turned) - 1)]
    placed = []
    for j in range((span + MOVE) // LANES):
        value = zero
        for h in range(MOVE // LANES):
            if 0 <= j - h < len(shifted):
                value = jnp.where(whole == h, shifted[j - h], value)
        placed.append(value.astype(jnp.bfloat16))
    pieces = length // LANES
    blank = zero.astype(jnp.bfloat16)
    for i in range(pieces):
        for j in range(len(placed) + pieces - 1):
            value = placed[j - i] if 0 <= j - i < len(placed) else blank
            spread[i * count : (i + 1) * count, j * LANES : (j + 1) * LANES] = value
    products = lax.dot_general(
        spread[...],
        hankel_ref[:, : spread.shape[1]],
        (((1,), (1,)), ((), ())),
        preferred_element_type=jnp.float32,
    )
    update = jnp.concatenate(
        [products[i * count : (i + 1) * count] for i in range(pieces)], axis=1
    )
    normal = update * lax.rsqrt(jnp.mean(update * update, axis=1, keepdims=True) + 1e-06)
    usable_here = jnp.broadcast_to(mask_ref[0], (count, length)) == 1
    initial = templates_ref[...].astype(jnp.float32)
    updated_ref[...] = jnp.where(usable_here, normal, initial).astype(jnp.bfloat16)


def body(traces, templates, moveouts, channel_mask, owner_slot):
    count, _, length = templates.shape
    win = traces.shape[1]
    span = win - MOVE - length
    stations = lax.axis_size("sta")
    owned = count // stations
    own_templates = templates.reshape(count, length)
    moves = moveouts.reshape(1, count)
    slots = owner_slot.reshape(1, count)
    scalar = pl.BlockSpec(memory_space=pltpu.SMEM)
    vector = pl.BlockSpec(memory_space=pltpu.VMEM)
    total, lagged = pl.pallas_call(
        functools.partial(forward_kernel, span),
        out_shape=(
            jax.ShapeDtypeStruct((count, span + LANES), jnp.float32),
            jax.ShapeDtypeStruct((LANES, win), jnp.bfloat16),
        ),
        in_specs=[scalar, vector, vector, vector],
        out_specs=(vector, vector),
        name="forward",
    )(channel_mask, traces, own_templates, moves)
    step = 1
    while step < stations:
        pairs = [(i, i ^ step) for i in range(stations)]
        total = total + lax.ppermute(total, "sta", pairs)
        step *= 2
    updated, own = pl.pallas_call(
        functools.partial(adjoint_kernel, span, owned),
        out_shape=(
            jax.ShapeDtypeStruct((count, length), jnp.bfloat16),
            jax.ShapeDtypeStruct((owned, span), jnp.bfloat16),
        ),
        in_specs=[scalar] + [vector] * 5,
        out_specs=(vector, vector),
        scratch_shapes=[
            pltpu.VMEM((count * length // LANES, win - LANES), jnp.bfloat16),
        ],
        name="adjoint",
    )(channel_mask, total, lagged, own_templates, moves, slots)
    return (updated.reshape(count, 1, length), own)


def solution(mesh):
    placed = (
        P(("grp", "sta"), None),
        P(None, ("grp", "sta"), None),
        P(None, ("grp", "sta")),
        P(("grp", "sta")),
        P(),
    )
    return jax.shard_map(
        body,
        mesh=mesh,
        in_specs=placed,
        out_specs=(P(None, ("grp", "sta"), None), P(("grp", "sta"), None)),
        check_vma=False,
    )
```

```python
import functools

import jax
import jax.numpy as jnp
from jax import lax
from jax.experimental import pallas as pl
from jax.experimental.pallas import tpu as pltpu
from jax.sharding import PartitionSpec as P

MOVE = 512
LANES = 128


def side(stations):
    index = lax.axis_index("sta")
    parity = index & 1
    for bit in range(1, stations.bit_length() - 1):
        parity = parity ^ ((index >> bit) & 1)
    return parity


def half_of(rows, which):
    half = rows.shape[0] // 2
    return jnp.where(which == 0, rows[:half], rows[half:])


def column(row):
    n = row.shape[1]
    wide = jnp.broadcast_to(row.astype(jnp.float32), (n, n))
    here = lax.broadcasted_iota(jnp.int32, (n, n), 0) == lax.broadcasted_iota(jnp.int32, (n, n), 1)
    return jnp.sum(jnp.where(here, wide, 0.0), axis=1, keepdims=True).astype(jnp.int32)


def blocks_of(value):
    return [value[:, i : i + LANES] for i in range(0, value.shape[1], LANES)]


def hankel(trace):
    win = trace.shape[1]
    base = jnp.broadcast_to(trace.astype(jnp.float32), (8, win))
    row = lax.broadcasted_iota(jnp.int32, (8, win), 0)
    for step in (1, 2, 4):
        base = jnp.where((row & step) != 0, pltpu.roll(base, win - step, 1), base)
    rows = [base] + [pltpu.roll(base, win - step, 1) for step in range(8, LANES, 8)]
    return jnp.concatenate(rows, axis=0).astype(jnp.bfloat16)


def shifts(moves_ref, which):
    rows = half_of(column(moves_ref[...]), which)
    moves = jnp.broadcast_to(rows, (rows.shape[0], LANES))
    return moves // LANES, moves % LANES


def correlate(span, which, mask_ref, lagged_ref, templates_ref, moves_ref, partial_ref):
    length = templates_ref.shape[1]
    widened = half_of(templates_ref[...].astype(jnp.float32), which)
    count = widened.shape[0]
    normed = widened * lax.rsqrt(jnp.sum(widened * widened, axis=1, keepdims=True) + 1e-06)
    pieces = blocks_of(normed)
    lags = span + MOVE
    products = jnp.dot(
        jnp.concatenate(pieces, axis=0).astype(jnp.bfloat16),
        lagged_ref[:, : lags + length - LANES],
        preferred_element_type=jnp.float32,
    )
    found = []
    for lag in range(0, lags, LANES):
        terms = [
            products[i * count : (i + 1) * count, lag + i * LANES : lag + (i + 1) * LANES]
            for i in range(len(pieces))
        ]
        found.append(functools.reduce(jnp.add, terms))
    whole, rest = shifts(moves_ref, which)
    lane = lax.broadcasted_iota(jnp.int32, (count, LANES), 1)
    source = (lane + rest) % LANES
    inside = lane + rest < LANES
    turned = []
    for j in range(span // LANES + 1):
        near = found[j]
        for h in range(1, MOVE // LANES):
            if j + h < len(found):
                near = jnp.where(whole == h, found[j + h], near)
        turned.append(jnp.take_along_axis(near, source, axis=1))
    weight = mask_ref[0].astype(jnp.float32)
    for j in range(span // LANES):
        partial_ref[:, j * LANES : (j + 1) * LANES] = (
            jnp.where(inside, turned[j], turned[j + 1]) * weight
        )
    partial_ref[:, span:] = jnp.full((count, LANES), weight, jnp.float32)


def sent_kernel(
    span, stations, mask_ref, trace_ref, templates_ref, moves_ref, slots_ref, partial_ref,
    lagged_ref, moves_out, slots_out,
):
    moves_out[...] = moves_ref[...]
    slots_out[...] = slots_ref[...]
    lagged_ref[...] = hankel(trace_ref[...])
    other = 1 - side(stations)
    correlate(span, other, mask_ref, lagged_ref, templates_ref, moves_ref, partial_ref)


def kept_kernel(span, stations, mask_ref, lagged_ref, templates_ref, moves_ref, partial_ref):
    own = side(stations)
    correlate(span, own, mask_ref, lagged_ref, templates_ref, moves_ref, partial_ref)


def cube_kernel(span, held_ref, got_ref, weights_ref):
    total = held_ref[...] + got_ref[...]
    stack = total[:, :span] * lax.rsqrt(jnp.maximum(total[:, span : span + 1], 1.0))
    weights_ref[...] = (stack * stack * stack).astype(jnp.bfloat16)


def adjoint(which, weights, mask_ref, lagged_ref, templates_ref, moves_ref, spread):
    length = templates_ref.shape[1]
    count, span = weights.shape
    whole, rest = shifts(moves_ref, which)
    lane = lax.broadcasted_iota(jnp.int32, (count, LANES), 1)
    source = (lane + LANES - rest) % LANES
    inside = lane >= rest
    zero = jnp.zeros((count, LANES), jnp.float32)
    turned = [jnp.take_along_axis(block, source, axis=1) for block in blocks_of(weights)]
    turned = [zero] + turned + [zero]
    shifted = [jnp.where(inside, turned[j + 1], turned[j]) for j in range(len(turned) - 1)]
    placed = []
    for j in range((span + MOVE) // LANES):
        value = zero
        for h in range(MOVE // LANES):
            if 0 <= j - h < len(shifted):
                value = jnp.where(whole == h, shifted[j - h], value)
        placed.append(value)
    pieces = length // LANES
    for j in range(len(placed) + pieces - 1):
        value = [placed[j - i] if 0 <= j - i < len(placed) else zero for i in range(pieces)]
        spread[:, j * LANES : (j + 1) * LANES] = jnp.concatenate(value, axis=0).astype(jnp.bfloat16)
    products = lax.dot_general(
        spread[...],
        lagged_ref[:, : spread.shape[1]],
        (((1,), (1,)), ((), ())),
        preferred_element_type=jnp.float32,
    )
    update = jnp.concatenate(
        [products[i * count : (i + 1) * count] for i in range(pieces)], axis=1
    )
    normal = update * lax.rsqrt(jnp.mean(update * update, axis=1, keepdims=True) + 1e-06)
    initial = half_of(templates_ref[...].astype(jnp.float32), which)
    return jnp.where(jnp.broadcast_to(mask_ref[0], normal.shape) == 1, normal, initial)


def owned_rows(owned, slots_ref, which, rows):
    slots = jnp.broadcast_to(half_of(column(slots_ref[...]), which), rows.shape)
    first = lax.axis_index("sta") * owned
    found = [
        jnp.sum(jnp.where(slots == first + j, rows, 0.0), axis=0, keepdims=True)
        for j in range(owned)
    ]
    return jnp.concatenate(found, axis=0)


def own_kernel(
    stations, owned, mask_ref, weights_ref, lagged_ref, templates_ref, moves_ref, slots_ref,
    updated_ref, own_ref, spread,
):
    wide = weights_ref[...].astype(jnp.float32)
    which = side(stations)
    updated_ref[...] = adjoint(
        which, wide, mask_ref, lagged_ref, templates_ref, moves_ref, spread
    )
    own_ref[...] = owned_rows(owned, slots_ref, which, wide)


def other_kernel(
    stations, owned, mask_ref, others_ref, ready_ref, found_ref, lagged_ref, templates_ref,
    moves_ref, slots_ref, updated_ref, own_ref, spread,
):
    which = side(stations)
    others = others_ref[...].astype(jnp.float32)
    ready = ready_ref[...]
    rows = found_ref[...] + owned_rows(owned, slots_ref, 1 - which, others)
    own_ref[...] = rows.astype(jnp.bfloat16)
    late = adjoint(1 - which, others, mask_ref, lagged_ref, templates_ref, moves_ref, spread)
    low = jnp.where(which == 0, ready, late)
    high = jnp.where(which == 0, late, ready)
    updated_ref[...] = jnp.concatenate([low, high], axis=0).astype(jnp.bfloat16)


def exchange(rows, step):
    stations = lax.axis_size("sta")
    return lax.ppermute(rows, "sta", [(i, i ^ step) for i in range(stations)])


def body(traces, templates, moveouts, channel_mask, owner_slot):
    count, _, length = templates.shape
    half = count // 2
    win = traces.shape[1]
    span = win - MOVE - length
    stations = lax.axis_size("sta")
    owned = count // stations
    own_templates = templates.reshape(count, length)
    moves = moveouts.reshape(1, count)
    slots = owner_slot.reshape(1, count)
    scalar = pl.BlockSpec(memory_space=pltpu.SMEM)
    vector = pl.BlockSpec(memory_space=pltpu.VMEM)
    near = functools.partial(pltpu.with_memory_space_constraint, memory_space=pltpu.VMEM)
    spread = [pltpu.VMEM((half * length // LANES, win - LANES), jnp.bfloat16)]
    work = pl.CostEstimate(
        flops=2 * count * length * win, bytes_accessed=LANES * win * 8, transcendentals=0
    )
    sent, lagged, near_moves, near_slots = pl.pallas_call(
        functools.partial(sent_kernel, span, stations),
        out_shape=(
            pltpu.VMEM((half, span + LANES), jnp.float32),
            pltpu.VMEM((LANES, win), jnp.bfloat16),
            pltpu.VMEM((1, count), jnp.int32),
            pltpu.VMEM((1, count), jnp.int32),
        ),
        in_specs=[scalar] + [vector] * 4,
        out_specs=(vector,) * 4,
        name="correlate_sent",
    )(channel_mask, traces, own_templates, moves, slots)
    kept = pl.pallas_call(
        functools.partial(kept_kernel, span, stations),
        out_shape=pltpu.VMEM((half, span + LANES), jnp.float32),
        in_specs=[scalar] + [vector] * 3,
        out_specs=vector,
        cost_estimate=work,
        name="correlate_kept",
    )(channel_mask, near(lagged), near(own_templates), near(near_moves))
    held, got = kept, exchange(sent, 1)
    steps = [1 << i for i in range(1, stations.bit_length() - 1)]
    for i in range(0, len(steps), 2):
        held = held + got
        pair = steps[i : i + 2]
        others = [step | 1 for step in pair] + [pair[0] | pair[-1]] * (len(pair) - 1)
        got = functools.reduce(jnp.add, [exchange(held, step) for step in others])
    weights = pl.pallas_call(
        functools.partial(cube_kernel, span),
        out_shape=pltpu.VMEM((half, span), jnp.bfloat16),
        in_specs=[vector] * 2,
        out_specs=vector,
        name="cube",
    )(near(held), near(got))
    ready, found = pl.pallas_call(
        functools.partial(own_kernel, stations, owned),
        out_shape=(
            pltpu.VMEM((half, length), jnp.float32),
            pltpu.VMEM((owned, span), jnp.float32),
        ),
        in_specs=[scalar] + [vector] * 5,
        out_specs=(vector, vector),
        scratch_shapes=spread,
        cost_estimate=work,
        name="adjoint_own",
    )(channel_mask, near(weights), near(lagged), near(own_templates), near(near_moves), near(near_slots))
    updated, own = pl.pallas_call(
        functools.partial(other_kernel, stations, owned),
        out_shape=(
            jax.ShapeDtypeStruct((count, length), jnp.bfloat16),
            jax.ShapeDtypeStruct((owned, span), jnp.bfloat16),
        ),
        in_specs=[scalar] + [vector] * 7,
        out_specs=(vector, vector),
        scratch_shapes=spread,
        name="adjoint_other",
    )(
        channel_mask, near(exchange(weights, 1)), near(ready), near(found), near(lagged),
        near(own_templates), near(near_moves), near(near_slots),
    )
    return (updated.reshape(count, 1, length), own)


def solution(mesh):
    placed = (
        P(("grp", "sta"), None),
        P(None, ("grp", "sta"), None),
        P(None, ("grp", "sta")),
        P(("grp", "sta")),
        P(),
    )
    return jax.shard_map(
        body,
        mesh=mesh,
        in_specs=placed,
        out_specs=(P(None, ("grp", "sta"), None), P(("grp", "sta"), None)),
        check_vma=False,
    )
```

```python
import functools

import jax
import jax.numpy as jnp
from jax import lax
from jax.experimental import pallas as pl
from jax.experimental.pallas import tpu as pltpu
from jax.sharding import PartitionSpec as P


MOVE = 512
LANES = 128


def side(stations):
    index = lax.axis_index("sta")
    parity = index & 1
    for bit in range(1, stations.bit_length() - 1):
        parity = parity ^ ((index >> bit) & 1)
    return parity


def half_of(rows, which):
    half = rows.shape[0] // 2
    return jnp.where(which == 0, rows[:half], rows[half:])


def column(row):
    n = row.shape[1]
    wide = jnp.broadcast_to(row.astype(jnp.float32), (n, n))
    here = lax.broadcasted_iota(jnp.int32, (n, n), 0) == lax.broadcasted_iota(jnp.int32, (n, n), 1)
    return jnp.sum(jnp.where(here, wide, 0.0), axis=1, keepdims=True).astype(jnp.int32)


def blocks_of(value):
    return [value[:, i : i + LANES] for i in range(0, value.shape[1], LANES)]


def hankel(trace):
    win = trace.shape[1]
    base = jnp.broadcast_to(trace.astype(jnp.float32), (8, win))
    row = lax.broadcasted_iota(jnp.int32, (8, win), 0)
    for step in (1, 2, 4):
        base = jnp.where((row & step) != 0, pltpu.roll(base, win - step, 1), base)
    rows = [base] + [pltpu.roll(base, win - step, 1) for step in range(8, LANES, 8)]
    return jnp.concatenate(rows, axis=0).astype(jnp.bfloat16)


def shifts(moves_ref, which):
    rows = half_of(column(moves_ref[...]), which)
    moves = jnp.broadcast_to(rows, (rows.shape[0], LANES))
    return moves // LANES, moves % LANES


def correlate(
    span, which, mask_ref, lagged_ref, templates_ref, moves_ref, partial_ref, moves_ready=None
):
    length = templates_ref.shape[1]
    widened = half_of(templates_ref[...].astype(jnp.float32), which)
    count = widened.shape[0]
    normed = widened * lax.rsqrt(jnp.sum(widened * widened, axis=1, keepdims=True) + 1e-06)
    pieces = blocks_of(normed)
    lags = span + MOVE
    products = jnp.dot(
        jnp.concatenate(pieces, axis=0).astype(jnp.bfloat16),
        lagged_ref[:, : lags + length - LANES],
        preferred_element_type=jnp.float32,
    )
    found = []
    for lag in range(0, lags, LANES):
        terms = [
            products[i * count : (i + 1) * count, lag + i * LANES : lag + (i + 1) * LANES]
            for i in range(len(pieces))
        ]
        found.append(functools.reduce(jnp.add, terms))
    if moves_ready is not None:
        moves_ready()
    whole, rest = shifts(moves_ref, which)
    lane = lax.broadcasted_iota(jnp.int32, (count, LANES), 1)
    source = (lane + rest) % LANES
    inside = lane + rest < LANES
    turned = []
    for j in range(span // LANES + 1):
        near = found[j]
        for h in range(1, MOVE // LANES):
            if j + h < len(found):
                near = jnp.where(whole == h, found[j + h], near)
        turned.append(jnp.take_along_axis(near, source, axis=1))
    weight = mask_ref[0].astype(jnp.float32)
    for j in range(span // LANES):
        partial_ref[:, j * LANES : (j + 1) * LANES] = (
            jnp.where(inside, turned[j], turned[j + 1]) * weight
        )
    partial_ref[:, span:] = jnp.full((count, LANES), weight, jnp.float32)


def lead_kernel(lead_ref):
    lead_ref[...] = jnp.ones_like(lead_ref)


def sent_kernel(
    span, stations, mask_ref, lead_ref, trace_ref, templates_ref, moves_far, slots_far,
    partial_ref, lagged_ref, moves_ref, slots_ref, arrived,
):
    del lead_ref
    moves_copy = pltpu.make_async_copy(moves_far, moves_ref, arrived.at[0])
    slots_copy = pltpu.make_async_copy(slots_far, slots_ref, arrived.at[1])

    @pl.when(lax.axis_index("sta") >= 0)
    def _():
        moves_copy.start()
        slots_copy.start()

    lagged_ref[...] = hankel(trace_ref[...])
    other = 1 - side(stations)
    correlate(
        span, other, mask_ref, lagged_ref, templates_ref, moves_ref, partial_ref, moves_copy.wait
    )
    slots_copy.wait()


def kept_kernel(span, stations, mask_ref, lagged_ref, templates_ref, moves_ref, partial_ref):
    own = side(stations)
    correlate(span, own, mask_ref, lagged_ref, templates_ref, moves_ref, partial_ref)


def cube_kernel(span, held_ref, got_ref, weights_ref):
    total = held_ref[...] + got_ref[...]
    stack = total[:, :span] * lax.rsqrt(jnp.maximum(total[:, span : span + 1], 1.0))
    weights_ref[...] = (stack * stack * stack).astype(jnp.bfloat16)


def prepare_kernel(
    stations, owned, lagged_ref, templates_ref, moves_ref, slots_ref, turned_ref, whole_ref,
    rest_ref, slots_out, initial_ref,
):
    turned_ref[...] = lagged_ref[...].astype(jnp.float32).T.astype(jnp.bfloat16)
    own = side(stations)
    templates = templates_ref[...].astype(jnp.float32)
    first = lax.axis_index("sta") * owned
    for place, which in enumerate((own, 1 - own)):
        whole_ref[place], rest_ref[place] = shifts(moves_ref, which)
        slots = half_of(column(slots_ref[...]), which) - first
        slots_out[place] = jnp.broadcast_to(slots, slots_out.shape[1:])
        initial_ref[place] = half_of(templates, which)


def adjoint(place, weights, mask_ref, turned_ref, whole_ref, rest_ref, initial_ref, spread):
    count, span = weights.shape
    length = initial_ref.shape[2]
    whole, rest = whole_ref[place], rest_ref[place]
    lane = lax.broadcasted_iota(jnp.int32, (count, LANES), 1)
    source = (lane + LANES - rest) % LANES
    inside = lane >= rest
    zero = jnp.zeros((count, LANES), jnp.float32)
    turned = [jnp.take_along_axis(block, source, axis=1) for block in blocks_of(weights)]
    turned = [zero] + turned + [zero]
    shifted = [jnp.where(inside, turned[j + 1], turned[j]) for j in range(len(turned) - 1)]
    placed = []
    for j in range((span + MOVE) // LANES):
        value = zero
        for h in range(MOVE // LANES):
            if 0 <= j - h < len(shifted):
                value = jnp.where(whole == h, shifted[j - h], value)
        placed.append(value)
    pieces = length // LANES
    for j in range(len(placed) + pieces - 1):
        value = [placed[j - i] if 0 <= j - i < len(placed) else zero for i in range(pieces)]
        spread[:, j * LANES : (j + 1) * LANES] = jnp.concatenate(value, axis=0).astype(jnp.bfloat16)
    products = jnp.dot(
        spread[...], turned_ref[: spread.shape[1], :], preferred_element_type=jnp.float32
    )
    update = jnp.concatenate(
        [products[i * count : (i + 1) * count] for i in range(pieces)], axis=1
    )
    normal = update * lax.rsqrt(jnp.mean(update * update, axis=1, keepdims=True) + 1e-06)
    usable = jnp.broadcast_to(mask_ref[0], normal.shape) == 1
    return jnp.where(usable, normal, initial_ref[place])


def owned_rows(owned, place, slots_ref, rows):
    slots = jnp.tile(slots_ref[place], (1, rows.shape[1] // LANES))
    found = [
        jnp.sum(jnp.where(slots == j, rows, 0.0), axis=0, keepdims=True) for j in range(owned)
    ]
    return jnp.concatenate(found, axis=0)


def own_kernel(
    owned, mask_ref, weights_ref, turned_ref, whole_ref, rest_ref, slots_ref, initial_ref,
    updated_ref, own_ref, spread,
):
    wide = weights_ref[...].astype(jnp.float32)
    updated_ref[...] = adjoint(
        0, wide, mask_ref, turned_ref, whole_ref, rest_ref, initial_ref, spread
    )
    own_ref[...] = owned_rows(owned, 0, slots_ref, wide)


def other_kernel(
    stations, owned, mask_ref, others_ref, ready_ref, found_ref, turned_ref, whole_ref,
    rest_ref, slots_ref, initial_ref, updated_ref, own_ref, spread,
):
    which = side(stations)
    others = others_ref[...].astype(jnp.float32)
    ready = ready_ref[...]
    rows = found_ref[...] + owned_rows(owned, 1, slots_ref, others)
    own_ref[...] = rows.astype(jnp.bfloat16)
    late = adjoint(1, others, mask_ref, turned_ref, whole_ref, rest_ref, initial_ref, spread)
    low = jnp.where(which == 0, ready, late)
    high = jnp.where(which == 0, late, ready)
    updated_ref[...] = jnp.concatenate([low, high], axis=0).astype(jnp.bfloat16)


def exchange(rows, step):
    stations = lax.axis_size("sta")
    return lax.ppermute(rows, "sta", [(i, i ^ step) for i in range(stations)])


def stages(stations):
    bits = [1 << i for i in range(1, stations.bit_length() - 1)]
    pairs = [bits[i : i + 2] for i in range(0, len(bits), 2)]
    return [
        [pair[0] | pair[1], pair[1] | 1, pair[0] | 1] if len(pair) == 2 else [pair[0] | 1]
        for pair in pairs
    ]


def whole_step(traces, templates, moveouts, channel_mask, owner_slot):
    count, _, length = templates.shape
    half = count // 2
    win = traces.shape[1]
    span = win - MOVE - length
    stations = lax.axis_size("sta")
    owned = count // stations
    own_templates = templates.reshape(count, length)
    moves = moveouts.reshape(1, count)
    slots = owner_slot.reshape(1, count)
    scalar = pl.BlockSpec(memory_space=pltpu.SMEM)
    vector = pl.BlockSpec(memory_space=pltpu.VMEM)
    near = functools.partial(pltpu.with_memory_space_constraint, memory_space=pltpu.VMEM)
    spread = [pltpu.VMEM((half * length // LANES, win - LANES), jnp.bfloat16)]
    work = pl.CostEstimate(
        flops=2 * count * length * win, bytes_accessed=LANES * win * 8, transcendentals=0
    )
    lead = pl.pallas_call(
        lead_kernel,
        out_shape=pltpu.VMEM((8, LANES), jnp.float32),
        out_specs=vector,
        cost_estimate=pl.CostEstimate(flops=10**9, bytes_accessed=10**7, transcendentals=0),
        name="lead",
    )()
    trace = near(traces)
    own_templates = near(own_templates)
    far = pl.BlockSpec(memory_space=pltpu.HBM)
    sent, lagged, moves, slots = pl.pallas_call(
        functools.partial(sent_kernel, span, stations),
        out_shape=(
            pltpu.VMEM((half, span + LANES), jnp.float32),
            pltpu.VMEM((LANES, win), jnp.bfloat16),
            pltpu.VMEM((1, count), jnp.int32),
            pltpu.VMEM((1, count), jnp.int32),
        ),
        in_specs=[scalar] + [vector] * 3 + [far] * 2,
        out_specs=(vector,) * 4,
        scratch_shapes=[pltpu.SemaphoreType.DMA((2,))],
        name="correlate_sent",
    )(channel_mask, near(lead), trace, own_templates, moves, slots)
    moves, slots = near(moves), near(slots)
    kept = pl.pallas_call(
        functools.partial(kept_kernel, span, stations),
        out_shape=pltpu.VMEM((half, span + LANES), jnp.float32),
        in_specs=[scalar] + [vector] * 3,
        out_specs=vector,
        cost_estimate=work,
        name="correlate_kept",
    )(channel_mask, near(lagged), own_templates, moves)
    ahead = pl.pallas_call(
        functools.partial(prepare_kernel, stations, owned),
        out_shape=(
            pltpu.VMEM((win, LANES), jnp.bfloat16),
            pltpu.VMEM((2, half, LANES), jnp.int32),
            pltpu.VMEM((2, half, LANES), jnp.int32),
            pltpu.VMEM((2, half, LANES), jnp.int32),
            pltpu.VMEM((2, half, length), jnp.float32),
        ),
        in_specs=[vector] * 4,
        out_specs=(vector,) * 5,
        cost_estimate=work,
        name="prepare",
    )(near(lagged), own_templates, moves, slots)
    ahead = [near(value) for value in ahead]
    held, got = kept, exchange(sent, 1)
    for hops in stages(stations):
        held = held + got
        parts = []
        for step in hops:
            parts.append(exchange(held, step))
        got = functools.reduce(jnp.add, parts)
    weights = pl.pallas_call(
        functools.partial(cube_kernel, span),
        out_shape=pltpu.VMEM((half, span), jnp.bfloat16),
        in_specs=[vector] * 2,
        out_specs=vector,
        name="cube",
    )(near(held), near(got))
    ready, found = pl.pallas_call(
        functools.partial(own_kernel, owned),
        out_shape=(
            pltpu.VMEM((half, length), jnp.float32),
            pltpu.VMEM((owned, span), jnp.float32),
        ),
        in_specs=[scalar] + [vector] * 6,
        out_specs=(vector, vector),
        scratch_shapes=spread,
        cost_estimate=work,
        name="adjoint_own",
    )(channel_mask, near(weights), *ahead)
    updated, own = pl.pallas_call(
        functools.partial(other_kernel, stations, owned),
        out_shape=(
            jax.ShapeDtypeStruct((count, length), jnp.bfloat16),
            jax.ShapeDtypeStruct((owned, span), jnp.bfloat16),
        ),
        in_specs=[scalar] + [vector] * 8,
        out_specs=(vector, vector),
        scratch_shapes=spread,
        name="adjoint_other",
    )(channel_mask, near(exchange(weights, 1)), near(ready), near(found), *ahead)
    return (updated.reshape(count, 1, length), own)


def solution(mesh):
    placed = (
        P(("grp", "sta"), None),
        P(None, ("grp", "sta"), None),
        P(None, ("grp", "sta")),
        P(("grp", "sta")),
        P(),
    )
    return jax.shard_map(
        whole_step,
        mesh=mesh,
        in_specs=placed,
        out_specs=(P(None, ("grp", "sta"), None), P(("grp", "sta"), None)),
        check_vma=False,
    )
```

```python
import functools

import jax
import jax.numpy as jnp
from jax import lax
from jax.experimental import pallas as pl
from jax.experimental.pallas import tpu as pltpu
from jax.sharding import PartitionSpec as P


MOVE = 512
LANES = 128


def side(stations):
    index = lax.axis_index("sta")
    parity = index & 1
    for bit in range(1, stations.bit_length() - 1):
        parity = parity ^ ((index >> bit) & 1)
    return parity


def half_of(rows, which):
    half = rows.shape[0] // 2
    return jnp.where(which == 0, rows[:half], rows[half:])


def column(row):
    n = row.shape[1]
    wide = jnp.broadcast_to(row.astype(jnp.float32), (n, n))
    here = lax.broadcasted_iota(jnp.int32, (n, n), 0) == lax.broadcasted_iota(jnp.int32, (n, n), 1)
    return jnp.sum(jnp.where(here, wide, 0.0), axis=1, keepdims=True).astype(jnp.int32)


def blocks_of(value):
    return [value[:, i : i + LANES] for i in range(0, value.shape[1], LANES)]


def lag(blocks, step, lane):
    turned = [pltpu.roll(block, LANES - step, 1) for block in blocks]
    kept = lane < LANES - step
    return [jnp.where(kept, t, n) for t, n in zip(turned, turned[1:] + turned[-1:])]


def hankel(trace):
    shape = (8, LANES)
    blocks = [jnp.broadcast_to(block, shape) for block in blocks_of(trace.astype(jnp.float32))]
    row, lane = (lax.broadcasted_iota(jnp.int32, shape, axis) for axis in (0, 1))
    for step in (1, 2, 4):
        odd = (row & step) != 0
        blocks = [jnp.where(odd, n, o) for n, o in zip(lag(blocks, step, lane), blocks)]
    pairs = zip(blocks, lag(blocks, 8, lane))
    blocks = [jnp.concatenate(pair, axis=0).astype(jnp.bfloat16) for pair in pairs]
    lane = lax.broadcasted_iota(jnp.int32, (16, LANES), 1)
    rows = [blocks] + [lag(blocks, step, lane) for step in range(16, LANES, 16)]
    return [jnp.concatenate(column, axis=0) for column in list(zip(*rows))[:-1]]


def shifts(moves_ref, which):
    rows = half_of(column(moves_ref[...]), which)
    moves = jnp.broadcast_to(rows, (rows.shape[0], LANES))
    return moves // LANES, moves % LANES


def correlate(span, which, mask_ref, tiles, templates_ref, moves_ref, partial_ref, moves_ready):
    widened = half_of(templates_ref[...].astype(jnp.float32), which)
    count = widened.shape[0]
    normed = widened * lax.rsqrt(jnp.sum(widened * widened, axis=1, keepdims=True) + 1e-06)
    pieces = blocks_of(normed)
    stacked = jnp.concatenate(pieces, axis=0).astype(jnp.bfloat16)
    lags = span + MOVE
    products = [jnp.dot(stacked, tile, preferred_element_type=jnp.float32) for tile in tiles]
    products = [block for product in products for block in blocks_of(product)]
    moves_ready()
    whole, rest = shifts(moves_ref, which)
    found = []
    for j in range(lags // LANES):
        terms = [products[j + i][i * count : (i + 1) * count] for i in range(len(pieces))]
        found.append(functools.reduce(jnp.add, terms))
    lane = lax.broadcasted_iota(jnp.int32, (count, LANES), 1)
    source = (lane + rest) % LANES
    inside = lane + rest < LANES
    turned = []
    for j in range(span // LANES + 1):
        near = found[j]
        for h in range(1, MOVE // LANES):
            if j + h < len(found):
                near = jnp.where(whole == h, found[j + h], near)
        turned.append(jnp.take_along_axis(near, source, axis=1))
    weight = mask_ref[0].astype(jnp.float32)
    for j in range(span // LANES):
        partial_ref[:, j * LANES : (j + 1) * LANES] = (
            jnp.where(inside, turned[j], turned[j + 1]) * weight
        )
    partial_ref[:, span:] = jnp.full((count, LANES), weight, jnp.float32)


def lead_kernel(lead_ref):
    lead_ref[...] = jnp.ones_like(lead_ref)


def sent_kernel(
    span, stations, mask_ref, lead_ref, trace_ref, templates_ref, moves_far, slots_far,
    partial_ref, lagged_ref, moves_ref, slots_ref, arrived,
):
    del lead_ref
    moves_copy = pltpu.make_async_copy(moves_far, moves_ref, arrived.at[0])
    slots_copy = pltpu.make_async_copy(slots_far, slots_ref, arrived.at[1])

    @pl.when(lax.axis_index("sta") >= 0)
    def _():
        moves_copy.start()
        slots_copy.start()

    blocks = hankel(trace_ref[...])
    tiles = [jnp.concatenate(blocks[i : i + 2], axis=1) for i in range(0, len(blocks), 2)]
    for i, tile in enumerate(tiles):
        lagged_ref[:, i * 2 * LANES : i * 2 * LANES + tile.shape[1]] = tile
    other = 1 - side(stations)
    correlate(
        span, other, mask_ref, tiles, templates_ref, moves_ref, partial_ref, moves_copy.wait
    )
    slots_copy.wait()


def kept_kernel(span, stations, mask_ref, lagged_ref, templates_ref, moves_ref, partial_ref):
    own = side(stations)
    tiles = [lagged_ref[...]]
    correlate(span, own, mask_ref, tiles, templates_ref, moves_ref, partial_ref, lambda: None)


def cube_kernel(span, held_ref, got_ref, weights_ref):
    total = held_ref[...] + got_ref[...]
    stack = total[:, :span] * lax.rsqrt(jnp.maximum(total[:, span : span + 1], 1.0))
    weights_ref[...] = (stack * stack * stack).astype(jnp.bfloat16)


def prepare_kernel(
    stations, owned, lagged_ref, templates_ref, moves_ref, slots_ref, turned_ref, whole_ref,
    rest_ref, slots_out, initial_ref,
):
    turned_ref[...] = lagged_ref[...].astype(jnp.float32).T.astype(jnp.bfloat16)
    own = side(stations)
    templates = templates_ref[...].astype(jnp.float32)
    first = lax.axis_index("sta") * owned
    for place, which in enumerate((own, 1 - own)):
        whole_ref[place], rest_ref[place] = shifts(moves_ref, which)
        slots = half_of(column(slots_ref[...]), which) - first
        slots_out[place] = jnp.broadcast_to(slots, slots_out.shape[1:])
        initial_ref[place] = half_of(templates, which)


def adjoint(place, weights, mask_ref, turned_ref, whole_ref, rest_ref, initial_ref, spread):
    count, span = weights.shape
    length = initial_ref.shape[2]
    whole, rest = whole_ref[place], rest_ref[place]
    lane = lax.broadcasted_iota(jnp.int32, (count, LANES), 1)
    source = (lane + LANES - rest) % LANES
    inside = lane >= rest
    zero = jnp.zeros((count, LANES), jnp.float32)
    turned = [jnp.take_along_axis(block, source, axis=1) for block in blocks_of(weights)]
    turned = [zero] + turned + [zero]
    shifted = [jnp.where(inside, turned[j + 1], turned[j]) for j in range(len(turned) - 1)]
    placed = []
    for j in range((span + MOVE) // LANES):
        value = zero
        for h in range(MOVE // LANES):
            if 0 <= j - h < len(shifted):
                value = jnp.where(whole == h, shifted[j - h], value)
        placed.append(value)
    pieces = length // LANES
    for j in range(len(placed) + pieces - 1):
        value = [placed[j - i] if 0 <= j - i < len(placed) else zero for i in range(pieces)]
        spread[:, j * LANES : (j + 1) * LANES] = jnp.concatenate(value, axis=0).astype(jnp.bfloat16)
    products = jnp.dot(
        spread[...], turned_ref[...], preferred_element_type=jnp.float32
    )
    update = jnp.concatenate(
        [products[i * count : (i + 1) * count] for i in range(pieces)], axis=1
    )
    normal = update * lax.rsqrt(jnp.mean(update * update, axis=1, keepdims=True) + 1e-06)
    usable = jnp.broadcast_to(mask_ref[0], normal.shape) == 1
    return jnp.where(usable, normal, initial_ref[place])


def owned_rows(owned, place, slots_ref, rows):
    slots = jnp.tile(slots_ref[place], (1, rows.shape[1] // LANES))
    found = [
        jnp.sum(jnp.where(slots == j, rows, 0.0), axis=0, keepdims=True) for j in range(owned)
    ]
    return jnp.concatenate(found, axis=0)


def own_kernel(
    owned, mask_ref, weights_ref, turned_ref, whole_ref, rest_ref, slots_ref, initial_ref,
    updated_ref, own_ref, spread,
):
    wide = weights_ref[...].astype(jnp.float32)
    updated_ref[...] = adjoint(
        0, wide, mask_ref, turned_ref, whole_ref, rest_ref, initial_ref, spread
    )
    own_ref[...] = owned_rows(owned, 0, slots_ref, wide)


def other_kernel(
    stations, owned, mask_ref, others_ref, ready_ref, found_ref, turned_ref, whole_ref,
    rest_ref, slots_ref, initial_ref, updated_ref, own_ref, spread,
):
    which = side(stations)
    others = others_ref[...].astype(jnp.float32)
    ready = ready_ref[...]
    rows = found_ref[...] + owned_rows(owned, 1, slots_ref, others)
    own_ref[...] = rows.astype(jnp.bfloat16)
    late = adjoint(1, others, mask_ref, turned_ref, whole_ref, rest_ref, initial_ref, spread)
    low = jnp.where(which == 0, ready, late)
    high = jnp.where(which == 0, late, ready)
    updated_ref[...] = jnp.concatenate([low, high], axis=0).astype(jnp.bfloat16)


def exchange(rows, step):
    stations = lax.axis_size("sta")
    return lax.ppermute(rows, "sta", [(i, i ^ step) for i in range(stations)])


def stages(stations):
    bits = [1 << i for i in range(1, stations.bit_length() - 1)]
    pairs = [bits[i : i + 2] for i in range(0, len(bits), 2)]
    return [
        [pair[0] | pair[1], pair[1] | 1, pair[0] | 1] if len(pair) == 2 else [pair[0] | 1]
        for pair in pairs
    ]


def whole_step(traces, templates, moveouts, channel_mask, owner_slot):
    count, _, length = templates.shape
    half = count // 2
    win = traces.shape[1]
    span = win - MOVE - length
    stations = lax.axis_size("sta")
    owned = count // stations
    own_templates = templates.reshape(count, length)
    moves = moveouts.reshape(1, count)
    slots = owner_slot.reshape(1, count)
    scalar = pl.BlockSpec(memory_space=pltpu.SMEM)
    vector = pl.BlockSpec(memory_space=pltpu.VMEM)
    near = functools.partial(pltpu.with_memory_space_constraint, memory_space=pltpu.VMEM)
    spread = [pltpu.VMEM((half * length // LANES, win - LANES), jnp.bfloat16)]
    work = pl.CostEstimate(
        flops=2 * count * length * win, bytes_accessed=LANES * win * 8, transcendentals=0
    )
    lead = pl.pallas_call(
        lead_kernel,
        out_shape=pltpu.VMEM((8, LANES), jnp.float32),
        out_specs=vector,
        cost_estimate=pl.CostEstimate(flops=10**9, bytes_accessed=10**7, transcendentals=0),
        name="lead",
    )()
    trace = near(traces)
    own_templates = near(own_templates)
    far = pl.BlockSpec(memory_space=pltpu.HBM)
    sent, lagged, moves, slots = pl.pallas_call(
        functools.partial(sent_kernel, span, stations),
        out_shape=(
            pltpu.VMEM((half, span + LANES), jnp.float32),
            pltpu.VMEM((LANES, win - LANES), jnp.bfloat16),
            pltpu.VMEM((1, count), jnp.int32),
            pltpu.VMEM((1, count), jnp.int32),
        ),
        in_specs=[scalar] + [vector] * 3 + [far] * 2,
        out_specs=(vector,) * 4,
        scratch_shapes=[pltpu.SemaphoreType.DMA((2,))],
        name="correlate_sent",
    )(channel_mask, near(lead), trace, own_templates, moves, slots)
    moves, slots = near(moves), near(slots)
    kept = pl.pallas_call(
        functools.partial(kept_kernel, span, stations),
        out_shape=pltpu.VMEM((half, span + LANES), jnp.float32),
        in_specs=[scalar] + [vector] * 3,
        out_specs=vector,
        cost_estimate=work,
        name="correlate_kept",
    )(channel_mask, near(lagged), own_templates, moves)
    ahead = pl.pallas_call(
        functools.partial(prepare_kernel, stations, owned),
        out_shape=(
            pltpu.VMEM((win - LANES, LANES), jnp.bfloat16),
            pltpu.VMEM((2, half, LANES), jnp.int32),
            pltpu.VMEM((2, half, LANES), jnp.int32),
            pltpu.VMEM((2, half, LANES), jnp.int32),
            pltpu.VMEM((2, half, length), jnp.float32),
        ),
        in_specs=[vector] * 4,
        out_specs=(vector,) * 5,
        cost_estimate=work,
        name="prepare",
    )(near(lagged), own_templates, moves, slots)
    ahead = [near(value) for value in ahead]
    held, got = kept, exchange(sent, 1)
    for hops in stages(stations):
        held = held + got
        parts = []
        for step in hops:
            parts.append(exchange(held, step))
        got = functools.reduce(jnp.add, parts)
    weights = pl.pallas_call(
        functools.partial(cube_kernel, span),
        out_shape=pltpu.VMEM((half, span), jnp.bfloat16),
        in_specs=[vector] * 2,
        out_specs=vector,
        name="cube",
    )(near(held), near(got))
    ready, found = pl.pallas_call(
        functools.partial(own_kernel, owned),
        out_shape=(
            pltpu.VMEM((half, length), jnp.float32),
            pltpu.VMEM((owned, span), jnp.float32),
        ),
        in_specs=[scalar] + [vector] * 6,
        out_specs=(vector, vector),
        scratch_shapes=spread,
        cost_estimate=work,
        name="adjoint_own",
    )(channel_mask, near(weights), *ahead)
    updated, own = pl.pallas_call(
        functools.partial(other_kernel, stations, owned),
        out_shape=(
            jax.ShapeDtypeStruct((count, length), jnp.bfloat16),
            jax.ShapeDtypeStruct((owned, span), jnp.bfloat16),
        ),
        in_specs=[scalar] + [vector] * 8,
        out_specs=(vector, vector),
        scratch_shapes=spread,
        name="adjoint_other",
    )(channel_mask, near(exchange(weights, 1)), near(ready), near(found), *ahead)
    return (updated.reshape(count, 1, length), own)


def solution(mesh):
    placed = (
        P(("grp", "sta"), None),
        P(None, ("grp", "sta"), None),
        P(None, ("grp", "sta")),
        P(("grp", "sta")),
        P(),
    )
    return jax.shard_map(
        whole_step,
        mesh=mesh,
        in_specs=placed,
        out_specs=(P(None, ("grp", "sta"), None), P(("grp", "sta"), None)),
        check_vma=False,
    )
```

```python
import functools

import jax
import jax.numpy as jnp
from jax import lax
from jax.experimental import pallas as pl
from jax.experimental.pallas import tpu as pltpu
from jax.sharding import PartitionSpec as P


MOVE = 512
LANES = 128


def side(stations):
    index = lax.axis_index("sta")
    parity = index & 1
    for bit in range(1, stations.bit_length() - 1):
        parity = parity ^ ((index >> bit) & 1)
    return parity


def half_of(rows, which):
    half = rows.shape[0] // 2
    return jnp.where(which == 0, rows[:half], rows[half:])


def column(row):
    n = row.shape[1]
    wide = jnp.broadcast_to(row.astype(jnp.float32), (n, n))
    here = lax.broadcasted_iota(jnp.int32, (n, n), 0) == lax.broadcasted_iota(jnp.int32, (n, n), 1)
    return jnp.sum(jnp.where(here, wide, 0.0), axis=1, keepdims=True).astype(jnp.int32)


def blocks_of(value):
    return [value[:, i : i + LANES] for i in range(0, value.shape[1], LANES)]


def lag(blocks, step, lane):
    turned = [pltpu.roll(block, LANES - step, 1) for block in blocks]
    kept = lane < LANES - step
    return [jnp.where(kept, t, n) for t, n in zip(turned, turned[1:] + turned[-1:])]


def hankel(trace):
    shape = (8, LANES)
    blocks = [jnp.broadcast_to(block, shape) for block in blocks_of(trace.astype(jnp.float32))]
    row, lane = (lax.broadcasted_iota(jnp.int32, shape, axis) for axis in (0, 1))
    for step in (1, 2, 4):
        odd = (row & step) != 0
        blocks = [jnp.where(odd, n, o) for n, o in zip(lag(blocks, step, lane), blocks)]
    pairs = zip(blocks, lag(blocks, 8, lane))
    blocks = [jnp.concatenate(pair, axis=0).astype(jnp.bfloat16) for pair in pairs]
    lane = lax.broadcasted_iota(jnp.int32, (16, LANES), 1)
    rows = [blocks] + [lag(blocks, step, lane) for step in range(16, LANES, 16)]
    return [jnp.concatenate(column, axis=0) for column in list(zip(*rows))[:-1]]


def shifts(moves_ref, which):
    rows = half_of(column(moves_ref[...]), which)
    moves = jnp.broadcast_to(rows, (rows.shape[0], LANES))
    return moves // LANES, moves % LANES


def correlate(span, which, mask_ref, tiles, templates_ref, moves_ref, partial_ref, moves_ready):
    widened = half_of(templates_ref[...].astype(jnp.float32), which)
    count = widened.shape[0]
    normed = widened * lax.rsqrt(jnp.sum(widened * widened, axis=1, keepdims=True) + 1e-06)
    pieces = blocks_of(normed)
    stacked = jnp.concatenate(pieces, axis=0).astype(jnp.bfloat16)
    lags = span + MOVE
    products = [jnp.dot(stacked, tile, preferred_element_type=jnp.float32) for tile in tiles]
    products = [block for product in products for block in blocks_of(product)]
    moves_ready()
    whole, rest = shifts(moves_ref, which)
    found = []
    for j in range(lags // LANES):
        terms = [products[j + i][i * count : (i + 1) * count] for i in range(len(pieces))]
        found.append(functools.reduce(jnp.add, terms))
    lane = lax.broadcasted_iota(jnp.int32, (count, LANES), 1)
    source = (lane + rest) % LANES
    inside = lane + rest < LANES
    turned = []
    for j in range(span // LANES + 1):
        near = found[j]
        for h in range(1, MOVE // LANES):
            if j + h < len(found):
                near = jnp.where(whole == h, found[j + h], near)
        turned.append(jnp.take_along_axis(near, source, axis=1))
    weight = mask_ref[0].astype(jnp.float32)
    for j in range(span // LANES):
        partial_ref[:, j * LANES : (j + 1) * LANES] = (
            jnp.where(inside, turned[j], turned[j + 1]) * weight
        )
    partial_ref[:, span:] = jnp.full((count, LANES), weight, jnp.float32)


def lead_kernel(lead_ref):
    lead_ref[...] = jnp.ones_like(lead_ref)


def sent_kernel(
    span, stations, mask_ref, lead_ref, trace_ref, templates_ref, moves_far, slots_far,
    partial_ref, lagged_ref, moves_ref, slots_ref, arrived,
):
    del lead_ref
    moves_copy = pltpu.make_async_copy(moves_far, moves_ref, arrived.at[0])
    slots_copy = pltpu.make_async_copy(slots_far, slots_ref, arrived.at[1])

    @pl.when(lax.axis_index("sta") >= 0)
    def _():
        moves_copy.start()
        slots_copy.start()

    blocks = hankel(trace_ref[...])
    tiles = [jnp.concatenate(blocks[i : i + 2], axis=1) for i in range(0, len(blocks), 2)]
    for i, tile in enumerate(tiles):
        lagged_ref[:, i * 2 * LANES : i * 2 * LANES + tile.shape[1]] = tile
    other = 1 - side(stations)
    correlate(
        span, other, mask_ref, tiles, templates_ref, moves_ref, partial_ref, moves_copy.wait
    )
    slots_copy.wait()


def kept_kernel(span, stations, mask_ref, lagged_ref, templates_ref, moves_ref, partial_ref):
    own = side(stations)
    tiles = [lagged_ref[...]]
    correlate(span, own, mask_ref, tiles, templates_ref, moves_ref, partial_ref, lambda: None)


def cube_kernel(span, held_ref, got_ref, weights_ref):
    total = held_ref[...] + got_ref[...]
    stack = total[:, :span] * lax.rsqrt(jnp.maximum(total[:, span : span + 1], 1.0))
    weights_ref[...] = (stack * stack * stack).astype(jnp.bfloat16)


def prepare_kernel(
    stations, owned, lagged_ref, templates_ref, moves_ref, slots_ref, turned_ref, whole_ref,
    rest_ref, slots_out, initial_ref,
):
    turned_ref[...] = lagged_ref[...].astype(jnp.float32).T.astype(jnp.bfloat16)
    own = side(stations)
    templates = templates_ref[...].astype(jnp.float32)
    first = lax.axis_index("sta") * owned
    for place, which in enumerate((own, 1 - own)):
        whole_ref[place], rest_ref[place] = shifts(moves_ref, which)
        slots = half_of(column(slots_ref[...]), which) - first
        slots_out[place] = jnp.broadcast_to(slots, slots_out.shape[1:])
        initial_ref[place] = half_of(templates, which)


def adjoint(place, weights, mask_ref, turned_ref, whole_ref, rest_ref, initial_ref, spread):
    count, span = weights.shape
    length = initial_ref.shape[2]
    whole, rest = whole_ref[place], rest_ref[place]
    lane = lax.broadcasted_iota(jnp.int32, (count, LANES), 1)
    source = (lane + LANES - rest) % LANES
    inside = lane >= rest
    zero = jnp.zeros((count, LANES), jnp.float32)
    turned = [jnp.take_along_axis(block, source, axis=1) for block in blocks_of(weights)]
    turned = [zero] + turned + [zero]
    shifted = [jnp.where(inside, turned[j + 1], turned[j]) for j in range(len(turned) - 1)]
    placed = []
    for j in range((span + MOVE) // LANES):
        value = zero
        for h in range(MOVE // LANES):
            if 0 <= j - h < len(shifted):
                value = jnp.where(whole == h, shifted[j - h], value)
        placed.append(value)
    pieces = length // LANES
    for j in range(len(placed) + pieces - 1):
        value = [placed[j - i] if 0 <= j - i < len(placed) else zero for i in range(pieces)]
        spread[:, j * LANES : (j + 1) * LANES] = jnp.concatenate(value, axis=0).astype(jnp.bfloat16)
    products = jnp.dot(
        spread[...], turned_ref[...], preferred_element_type=jnp.float32
    )
    update = jnp.concatenate(
        [products[i * count : (i + 1) * count] for i in range(pieces)], axis=1
    )
    normal = update * lax.rsqrt(jnp.mean(update * update, axis=1, keepdims=True) + 1e-06)
    usable = jnp.broadcast_to(mask_ref[0], normal.shape) == 1
    return jnp.where(usable, normal, initial_ref[place])


def owned_rows(owned, place, slots_ref, rows):
    slots = jnp.tile(slots_ref[place], (1, rows.shape[1] // LANES))
    found = [
        jnp.sum(jnp.where(slots == j, rows, 0.0), axis=0, keepdims=True) for j in range(owned)
    ]
    return jnp.concatenate(found, axis=0)


def own_kernel(
    owned, mask_ref, weights_ref, turned_ref, whole_ref, rest_ref, slots_ref, initial_ref,
    updated_ref, own_ref, spread,
):
    wide = weights_ref[...].astype(jnp.float32)
    updated_ref[...] = adjoint(
        0, wide, mask_ref, turned_ref, whole_ref, rest_ref, initial_ref, spread
    )
    own_ref[...] = owned_rows(owned, 0, slots_ref, wide)


def other_kernel(
    stations, owned, mask_ref, others_ref, ready_ref, found_ref, turned_ref, whole_ref,
    rest_ref, slots_ref, initial_ref, updated_ref, own_ref, spread,
):
    which = side(stations)
    others = others_ref[...].astype(jnp.float32)
    ready = ready_ref[...]
    rows = found_ref[...] + owned_rows(owned, 1, slots_ref, others)
    own_ref[...] = rows.astype(jnp.bfloat16)
    late = adjoint(1, others, mask_ref, turned_ref, whole_ref, rest_ref, initial_ref, spread)
    low = jnp.where(which == 0, ready, late)
    high = jnp.where(which == 0, late, ready)
    updated_ref[...] = jnp.concatenate([low, high], axis=0).astype(jnp.bfloat16)


def exchange(rows, steps):
    stations = lax.axis_size("sta")
    pairs = [(i, i ^ steps[i.bit_count() % 2]) for i in range(stations)]
    return lax.ppermute(rows, "sta", pairs)


def stages(stations):
    bits = [1 << i for i in range(1, stations.bit_length() - 1)]
    found = []
    for low, high in zip(bits[::2], bits[1::2]):
        low, high, both = low | 1, high | 1, low | high
        found.append([(both, low), (high, both), (low, high)])
    if len(bits) % 2:
        found.append([(bits[-1] | 1, bits[-1] | 1)])
    return found


def whole_step(traces, templates, moveouts, channel_mask, owner_slot):
    count, _, length = templates.shape
    half = count // 2
    win = traces.shape[1]
    span = win - MOVE - length
    stations = lax.axis_size("sta")
    owned = count // stations
    own_templates = templates.reshape(count, length)
    moves = moveouts.reshape(1, count)
    slots = owner_slot.reshape(1, count)
    scalar = pl.BlockSpec(memory_space=pltpu.SMEM)
    vector = pl.BlockSpec(memory_space=pltpu.VMEM)
    near = functools.partial(pltpu.with_memory_space_constraint, memory_space=pltpu.VMEM)
    spread = [pltpu.VMEM((half * length // LANES, win - LANES), jnp.bfloat16)]
    work = pl.CostEstimate(
        flops=2 * count * length * win, bytes_accessed=LANES * win * 8, transcendentals=0
    )
    lead = pl.pallas_call(
        lead_kernel,
        out_shape=pltpu.VMEM((8, LANES), jnp.float32),
        out_specs=vector,
        cost_estimate=pl.CostEstimate(flops=10**9, bytes_accessed=10**7, transcendentals=0),
        name="lead",
    )()
    trace = near(traces)
    own_templates = near(own_templates)
    far = pl.BlockSpec(memory_space=pltpu.HBM)
    sent, lagged, moves, slots = pl.pallas_call(
        functools.partial(sent_kernel, span, stations),
        out_shape=(
            pltpu.VMEM((half, span + LANES), jnp.float32),
            pltpu.VMEM((LANES, win - LANES), jnp.bfloat16),
            pltpu.VMEM((1, count), jnp.int32),
            pltpu.VMEM((1, count), jnp.int32),
        ),
        in_specs=[scalar] + [vector] * 3 + [far] * 2,
        out_specs=(vector,) * 4,
        scratch_shapes=[pltpu.SemaphoreType.DMA((2,))],
        name="correlate_sent",
    )(channel_mask, near(lead), trace, own_templates, moves, slots)
    moves, slots = near(moves), near(slots)
    kept = pl.pallas_call(
        functools.partial(kept_kernel, span, stations),
        out_shape=pltpu.VMEM((half, span + LANES), jnp.float32),
        in_specs=[scalar] + [vector] * 3,
        out_specs=vector,
        cost_estimate=work,
        name="correlate_kept",
    )(channel_mask, near(lagged), own_templates, moves)
    ahead = pl.pallas_call(
        functools.partial(prepare_kernel, stations, owned),
        out_shape=(
            pltpu.VMEM((win - LANES, LANES), jnp.bfloat16),
            pltpu.VMEM((2, half, LANES), jnp.int32),
            pltpu.VMEM((2, half, LANES), jnp.int32),
            pltpu.VMEM((2, half, LANES), jnp.int32),
            pltpu.VMEM((2, half, length), jnp.float32),
        ),
        in_specs=[vector] * 4,
        out_specs=(vector,) * 5,
        cost_estimate=work,
        name="prepare",
    )(near(lagged), own_templates, moves, slots)
    ahead = [near(value) for value in ahead]
    held, got = kept, exchange(sent, (1, 1))
    for hops in stages(stations):
        held = held + got
        parts = []
        for steps in hops:
            parts.append(exchange(held, steps))
        got = functools.reduce(jnp.add, parts)
    weights = pl.pallas_call(
        functools.partial(cube_kernel, span),
        out_shape=pltpu.VMEM((half, span), jnp.bfloat16),
        in_specs=[vector] * 2,
        out_specs=vector,
        name="cube",
    )(near(held), near(got))
    ready, found = pl.pallas_call(
        functools.partial(own_kernel, owned),
        out_shape=(
            pltpu.VMEM((half, length), jnp.float32),
            pltpu.VMEM((owned, span), jnp.float32),
        ),
        in_specs=[scalar] + [vector] * 6,
        out_specs=(vector, vector),
        scratch_shapes=spread,
        cost_estimate=work,
        name="adjoint_own",
    )(channel_mask, near(weights), *ahead)
    updated, own = pl.pallas_call(
        functools.partial(other_kernel, stations, owned),
        out_shape=(
            jax.ShapeDtypeStruct((count, length), jnp.bfloat16),
            jax.ShapeDtypeStruct((owned, span), jnp.bfloat16),
        ),
        in_specs=[scalar] + [vector] * 8,
        out_specs=(vector, vector),
        scratch_shapes=spread,
        name="adjoint_other",
    )(channel_mask, near(exchange(weights, (1, 1))), near(ready), near(found), *ahead)
    return (updated.reshape(count, 1, length), own)


def solution(mesh):
    placed = (
        P(("grp", "sta"), None),
        P(None, ("grp", "sta"), None),
        P(None, ("grp", "sta")),
        P(("grp", "sta")),
        P(),
    )
    return jax.shard_map(
        whole_step,
        mesh=mesh,
        in_specs=placed,
        out_specs=(P(None, ("grp", "sta"), None), P(("grp", "sta"), None)),
        check_vma=False,
    )
```

```python
import functools

import jax
import jax.numpy as jnp
from jax import lax
from jax.experimental import pallas as pl
from jax.experimental.pallas import tpu as pltpu
from jax.sharding import PartitionSpec as P


MOVE = 512
LANES = 128


def side(stations):
    index = lax.axis_index("sta")
    parity = index & 1
    for bit in range(1, stations.bit_length() - 1):
        parity = parity ^ ((index >> bit) & 1)
    return parity


def half_of(rows, which):
    half = rows.shape[0] // 2
    return jnp.where(which == 0, rows[:half], rows[half:])


def column(row):
    n = row.shape[1]
    wide = jnp.broadcast_to(row.astype(jnp.float32), (n, n))
    here = lax.broadcasted_iota(jnp.int32, (n, n), 0) == lax.broadcasted_iota(jnp.int32, (n, n), 1)
    return jnp.sum(jnp.where(here, wide, 0.0), axis=1, keepdims=True).astype(jnp.int32)


def blocks_of(value):
    return [value[:, i : i + LANES] for i in range(0, value.shape[1], LANES)]


def lag(blocks, step, lane):
    turned = [pltpu.roll(block, LANES - step, 1) for block in blocks]
    kept = lane < LANES - step
    return [jnp.where(kept, t, n) for t, n in zip(turned, turned[1:] + turned[-1:])]


def hankel(trace):
    shape = (8, LANES)
    blocks = [jnp.broadcast_to(block, shape) for block in blocks_of(trace.astype(jnp.float32))]
    row, lane = (lax.broadcasted_iota(jnp.int32, shape, axis) for axis in (0, 1))
    for step in (1, 2, 4):
        odd = (row & step) != 0
        blocks = [jnp.where(odd, n, o) for n, o in zip(lag(blocks, step, lane), blocks)]
    pairs = zip(blocks, lag(blocks, 8, lane))
    blocks = [jnp.concatenate(pair, axis=0).astype(jnp.bfloat16) for pair in pairs]
    lane = lax.broadcasted_iota(jnp.int32, (16, LANES), 1)
    rows = [blocks] + [lag(blocks, step, lane) for step in range(16, LANES, 16)]
    return [jnp.concatenate(column, axis=0) for column in list(zip(*rows))[:-1]]


def shifts(moves_ref, which):
    rows = half_of(column(moves_ref[...]), which)
    moves = jnp.broadcast_to(rows, (rows.shape[0], LANES))
    return moves // LANES, moves % LANES


def correlate(span, which, mask_ref, tiles, templates_ref, moves_ref, partial_ref, moves_ready):
    widened = half_of(templates_ref[...].astype(jnp.float32), which)
    count = widened.shape[0]
    normed = widened * lax.rsqrt(jnp.sum(widened * widened, axis=1, keepdims=True) + 1e-06)
    pieces = blocks_of(normed)
    stacked = jnp.concatenate(pieces, axis=0).astype(jnp.bfloat16)
    lags = span + MOVE
    products = [jnp.dot(stacked, tile, preferred_element_type=jnp.float32) for tile in tiles]
    products = [block for product in products for block in blocks_of(product)]
    moves_ready()
    whole, rest = shifts(moves_ref, which)
    found = []
    for j in range(lags // LANES):
        terms = [products[j + i][i * count : (i + 1) * count] for i in range(len(pieces))]
        found.append(functools.reduce(jnp.add, terms))
    lane = lax.broadcasted_iota(jnp.int32, (count, LANES), 1)
    source = (lane + rest) % LANES
    inside = lane + rest < LANES
    turned = []
    for j in range(span // LANES + 1):
        near = found[j]
        for h in range(1, MOVE // LANES):
            if j + h < len(found):
                near = jnp.where(whole == h, found[j + h], near)
        turned.append(jnp.take_along_axis(near, source, axis=1))
    weight = mask_ref[0].astype(jnp.float32)
    for j in range(span // LANES):
        partial_ref[:, j * LANES : (j + 1) * LANES] = (
            jnp.where(inside, turned[j], turned[j + 1]) * weight
        )
    partial_ref[:, span:] = jnp.full((count, LANES), weight, jnp.float32)


def lead_kernel(lead_ref):
    lead_ref[...] = jnp.ones_like(lead_ref)


def sent_kernel(
    span, stations, mask_ref, lead_ref, trace_ref, templates_ref, moves_far, slots_far,
    partial_ref, lagged_ref, moves_ref, slots_ref, arrived,
):
    del lead_ref
    moves_copy = pltpu.make_async_copy(moves_far, moves_ref, arrived.at[0])
    slots_copy = pltpu.make_async_copy(slots_far, slots_ref, arrived.at[1])

    @pl.when(lax.axis_index("sta") >= 0)
    def _():
        moves_copy.start()
        slots_copy.start()

    blocks = hankel(trace_ref[...])
    tiles = [jnp.concatenate(blocks[i : i + 2], axis=1) for i in range(0, len(blocks), 2)]
    for i, tile in enumerate(tiles):
        lagged_ref[:, i * 2 * LANES : i * 2 * LANES + tile.shape[1]] = tile
    other = 1 - side(stations)
    correlate(
        span, other, mask_ref, tiles, templates_ref, moves_ref, partial_ref, moves_copy.wait
    )
    slots_copy.wait()


def kept_kernel(span, stations, mask_ref, lagged_ref, templates_ref, moves_ref, partial_ref):
    own = side(stations)
    tiles = [lagged_ref[...]]
    correlate(span, own, mask_ref, tiles, templates_ref, moves_ref, partial_ref, lambda: None)


def cube_kernel(span, held_ref, got_ref, weights_ref):
    total = held_ref[...] + got_ref[...]
    stack = total[:, :span] * lax.rsqrt(jnp.maximum(total[:, span : span + 1], 1.0))
    weights_ref[...] = (stack * stack * stack).astype(jnp.bfloat16)


def prepare_kernel(
    stations, owned, lagged_ref, templates_ref, moves_ref, slots_ref, turned_ref, whole_ref,
    rest_ref, slots_out, initial_ref,
):
    turned = lagged_ref[...].astype(jnp.float32).T.astype(jnp.bfloat16)
    turned_ref[:, :LANES] = turned[:-LANES]
    turned_ref[:, LANES:] = turned[LANES:]
    own = side(stations)
    templates = templates_ref[...].astype(jnp.float32)
    first = lax.axis_index("sta") * owned
    for place, which in enumerate((own, 1 - own)):
        whole_ref[place], rest_ref[place] = shifts(moves_ref, which)
        slots = half_of(column(slots_ref[...]), which) - first
        slots_out[place] = jnp.broadcast_to(slots, slots_out.shape[1:])
        initial_ref[place] = half_of(templates, which)


def adjoint(place, weights, mask_ref, turned_ref, whole_ref, rest_ref, initial_ref, spread):
    count, span = weights.shape
    length = initial_ref.shape[2]
    whole, rest = whole_ref[place], rest_ref[place]
    lane = lax.broadcasted_iota(jnp.int32, (count, LANES), 1)
    source = (lane + LANES - rest) % LANES
    inside = lane >= rest
    zero = jnp.zeros((count, LANES), jnp.float32)
    turned = [jnp.take_along_axis(block, source, axis=1) for block in blocks_of(weights)]
    turned = [zero] + turned + [zero]
    shifted = [jnp.where(inside, turned[j + 1], turned[j]) for j in range(len(turned) - 1)]
    placed = []
    for j in range((span + MOVE) // LANES):
        value = zero
        for h in range(MOVE // LANES):
            if 0 <= j - h < len(shifted):
                value = jnp.where(whole == h, shifted[j - h], value)
        placed.append(value)
    pieces = length // LANES // 2
    for j in range(len(placed) + 2 * pieces - 2):
        value = [placed[j - 2 * i] if 0 <= j - 2 * i < len(placed) else zero for i in range(pieces)]
        spread[:, j * LANES : (j + 1) * LANES] = jnp.concatenate(value, axis=0).astype(jnp.bfloat16)
    products = jnp.dot(spread[...], turned_ref[...], preferred_element_type=jnp.float32)
    update = jnp.concatenate(
        [products[i * count : (i + 1) * count] for i in range(pieces)], axis=1
    )
    normal = update * lax.rsqrt(jnp.mean(update * update, axis=1, keepdims=True) + 1e-06)
    usable = jnp.broadcast_to(mask_ref[0], normal.shape) == 1
    return jnp.where(usable, normal, initial_ref[place])


def owned_rows(owned, place, slots_ref, rows):
    slots = jnp.tile(slots_ref[place], (1, rows.shape[1] // LANES))
    found = [
        jnp.sum(jnp.where(slots == j, rows, 0.0), axis=0, keepdims=True) for j in range(owned)
    ]
    return jnp.concatenate(found, axis=0)


def own_kernel(
    owned, mask_ref, weights_ref, turned_ref, whole_ref, rest_ref, slots_ref, initial_ref,
    updated_ref, own_ref, spread,
):
    wide = weights_ref[...].astype(jnp.float32)
    updated_ref[...] = adjoint(
        0, wide, mask_ref, turned_ref, whole_ref, rest_ref, initial_ref, spread
    )
    own_ref[...] = owned_rows(owned, 0, slots_ref, wide)


def other_kernel(
    stations, owned, mask_ref, others_ref, ready_ref, found_ref, turned_ref, whole_ref,
    rest_ref, slots_ref, initial_ref, updated_ref, own_ref, spread,
):
    which = side(stations)
    others = others_ref[...].astype(jnp.float32)
    ready = ready_ref[...]
    rows = found_ref[...] + owned_rows(owned, 1, slots_ref, others)
    own_ref[...] = rows.astype(jnp.bfloat16)
    late = adjoint(1, others, mask_ref, turned_ref, whole_ref, rest_ref, initial_ref, spread)
    low = jnp.where(which == 0, ready, late)
    high = jnp.where(which == 0, late, ready)
    updated_ref[...] = jnp.concatenate([low, high], axis=0).astype(jnp.bfloat16)


def exchange(rows, steps):
    stations = lax.axis_size("sta")
    pairs = [(i, i ^ steps[i.bit_count() % 2]) for i in range(stations)]
    return lax.ppermute(rows, "sta", pairs)


def stages(stations):
    bits = [1 << i for i in range(1, stations.bit_length() - 1)]
    found = []
    for low, high in zip(bits[::2], bits[1::2]):
        low, high, both = low | 1, high | 1, low | high
        found.append([(both, low), (high, both), (low, high)])
    if len(bits) % 2:
        found.append([(bits[-1] | 1, bits[-1] | 1)])
    return found


def whole_step(traces, templates, moveouts, channel_mask, owner_slot):
    count, _, length = templates.shape
    half = count // 2
    win = traces.shape[1]
    span = win - MOVE - length
    stations = lax.axis_size("sta")
    owned = count // stations
    own_templates = templates.reshape(count, length)
    moves = moveouts.reshape(1, count)
    slots = owner_slot.reshape(1, count)
    scalar = pl.BlockSpec(memory_space=pltpu.SMEM)
    vector = pl.BlockSpec(memory_space=pltpu.VMEM)
    near = functools.partial(pltpu.with_memory_space_constraint, memory_space=pltpu.VMEM)
    spread = [pltpu.VMEM((half * length // LANES // 2, win - 2 * LANES), jnp.bfloat16)]
    work = pl.CostEstimate(
        flops=2 * count * length * win, bytes_accessed=LANES * win * 8, transcendentals=0
    )
    lead = pl.pallas_call(
        lead_kernel,
        out_shape=pltpu.VMEM((8, LANES), jnp.float32),
        out_specs=vector,
        cost_estimate=pl.CostEstimate(flops=10**9, bytes_accessed=10**7, transcendentals=0),
        name="lead",
    )()
    trace = near(traces)
    own_templates = near(own_templates)
    far = pl.BlockSpec(memory_space=pltpu.HBM)
    sent, lagged, moves, slots = pl.pallas_call(
        functools.partial(sent_kernel, span, stations),
        out_shape=(
            pltpu.VMEM((half, span + LANES), jnp.float32),
            pltpu.VMEM((LANES, win - LANES), jnp.bfloat16),
            pltpu.VMEM((1, count), jnp.int32),
            pltpu.VMEM((1, count), jnp.int32),
        ),
        in_specs=[scalar] + [vector] * 3 + [far] * 2,
        out_specs=(vector,) * 4,
        scratch_shapes=[pltpu.SemaphoreType.DMA((2,))],
        name="correlate_sent",
    )(channel_mask, near(lead), trace, own_templates, moves, slots)
    moves, slots = near(moves), near(slots)
    kept = pl.pallas_call(
        functools.partial(kept_kernel, span, stations),
        out_shape=pltpu.VMEM((half, span + LANES), jnp.float32),
        in_specs=[scalar] + [vector] * 3,
        out_specs=vector,
        cost_estimate=work,
        name="correlate_kept",
    )(channel_mask, near(lagged), own_templates, moves)
    ahead = pl.pallas_call(
        functools.partial(prepare_kernel, stations, owned),
        out_shape=(
            pltpu.VMEM((win - 2 * LANES, 2 * LANES), jnp.bfloat16),
            pltpu.VMEM((2, half, LANES), jnp.int32),
            pltpu.VMEM((2, half, LANES), jnp.int32),
            pltpu.VMEM((2, half, LANES), jnp.int32),
            pltpu.VMEM((2, half, length), jnp.float32),
        ),
        in_specs=[vector] * 4,
        out_specs=(vector,) * 5,
        cost_estimate=work,
        name="prepare",
    )(near(lagged), own_templates, moves, slots)
    ahead = [near(value) for value in ahead]
    held, got = kept, exchange(sent, (1, 1))
    for hops in stages(stations):
        held = held + got
        parts = []
        for steps in hops:
            parts.append(exchange(held, steps))
        got = functools.reduce(jnp.add, parts)
    weights = pl.pallas_call(
        functools.partial(cube_kernel, span),
        out_shape=pltpu.VMEM((half, span), jnp.bfloat16),
        in_specs=[vector] * 2,
        out_specs=vector,
        name="cube",
    )(near(held), near(got))
    ready, found = pl.pallas_call(
        functools.partial(own_kernel, owned),
        out_shape=(
            pltpu.VMEM((half, length), jnp.float32),
            pltpu.VMEM((owned, span), jnp.float32),
        ),
        in_specs=[scalar] + [vector] * 6,
        out_specs=(vector, vector),
        scratch_shapes=spread,
        cost_estimate=work,
        name="adjoint_own",
    )(channel_mask, near(weights), *ahead)
    updated, own = pl.pallas_call(
        functools.partial(other_kernel, stations, owned),
        out_shape=(
            jax.ShapeDtypeStruct((count, length), jnp.bfloat16),
            jax.ShapeDtypeStruct((owned, span), jnp.bfloat16),
        ),
        in_specs=[scalar] + [vector] * 8,
        out_specs=(vector, vector),
        scratch_shapes=spread,
        name="adjoint_other",
    )(channel_mask, near(exchange(weights, (1, 1))), near(ready), near(found), *ahead)
    return (updated.reshape(count, 1, length), own)


def solution(mesh):
    placed = (
        P(("grp", "sta"), None),
        P(None, ("grp", "sta"), None),
        P(None, ("grp", "sta")),
        P(("grp", "sta")),
        P(),
    )
    return jax.shard_map(
        whole_step,
        mesh=mesh,
        in_specs=placed,
        out_specs=(P(None, ("grp", "sta"), None), P(("grp", "sta"), None)),
        check_vma=False,
    )
```
